256 devices in a mesh: rows: 64 (over z, x, core), rep: 4 (over y).
Axes of the slice: x: 4, y: 4, z: 8, core: 2. Of those that a mesh axis runs over, the one named last changes fastest.
Arguments:
- embeddings: bfloat16 [262144, 1024], P(('rows', 'rep')), may hold values from -0.25 to 0.25
- assignments: int32 [262144], P(('rows', 'rep')), may hold values from 0 to 65535, as said below
- old_centroids: bfloat16 [65536, 1024], P('rows'), may hold values from -0.25 to 0.25
- prior_counts: int32 [65536], P('rows'), may hold values from 1 to 8
Outputs:
- centroids: bfloat16 [65536, 1024], P('rows')
- row_score: float32 [262144], P(('rows', 'rep'))
The draws below stay inside these ranges and needn't reach their ends.
Inputs may be any that keep to these rules, and one draw needn't show every extreme that they name: Within each device's aligned block of 1024 rows the assignments never fall. Cluster k belongs to owner k // 1024; in every block at most 32 rows belong to one owner, and some owner receives exactly 32 of them.
All inputs are finite; a program needn't handle non-finite values.
Results may differ from the reference program's by a relative error of at most 0.0028.
Values may be sent and summed in bfloat16 or wider, within the bound.
A program may use at most 64 MiB of HBM per device.

```python
import jax
import jax.numpy as jnp
from jax import lax

D = 1024
CLUSTERS = 65536
ROW_DEV = 1024
OWNERS = 64
BLOCKS = 256
K_OWN = 1024
CAP = 32
ROWS_ALL = 262144


def draw_assign_block(key, hot_ids):
    k_one, k_two, k_three, k_four, k_five = jax.random.split(key, 5)
    half = CAP // 2
    spread = jax.random.randint(k_one, (OWNERS // 2,), 0, half + 1)
    spread = spread.at[0].set(half)
    load = jnp.concatenate([half + spread, half - spread])
    order = jax.random.permutation(k_two, OWNERS)
    loads = jnp.zeros((OWNERS,), jnp.int32).at[order].set(load.astype(jnp.int32))
    ends = jnp.cumsum(loads)
    position = jnp.arange(ROW_DEV, dtype=jnp.int32)
    owner_of = jnp.sum((position[:, None] >= ends[None, :]).astype(jnp.int32), axis=1)
    coin = jax.random.randint(k_three, (ROW_DEV,), 0, 2)
    pick = jax.random.randint(k_four, (ROW_DEV,), 0, 16)
    drawn = jax.random.randint(k_five, (ROW_DEV,), 0, K_OWN)
    hot_choice = hot_ids[owner_of, pick]
    local = jnp.where(coin == 1, hot_choice, drawn)
    return jnp.sort(owner_of * K_OWN + local).astype(jnp.int32)


def draw_assignments(key, part):
    hot_ids = jax.random.randint(jax.random.fold_in(key, 7), (OWNERS, 16), 0, K_OWN)
    keys = jax.random.split(jax.random.fold_in(key, 11), BLOCKS)
    blocks = jax.vmap(lambda one: draw_assign_block(one, hot_ids))(keys)
    return blocks.reshape(-1).astype(jnp.int32)


def place_ends(drawn, own_key, least, largest):
    longest = drawn.shape.index(max(drawn.shape))
    spots = []
    for shift in (0, 1):
        where = [jax.random.randint(jax.random.fold_in(own_key, axis), (), 0, length) for axis, length in enumerate(drawn.shape)]
        where[longest] = (where[longest] + shift) % drawn.shape[longest]
        spots.append(tuple(where))
    return drawn.at[spots[0]].set(least).at[spots[1]].set(largest)


def shard_levels(stream_key, shape, cuts, low, top_value):
    level, own = 1.0, jax.random.fold_in(stream_key, 6)
    for dim, parts in cuts:
        heights = jnp.exp(jax.random.uniform(jax.random.fold_in(own, dim), (parts,), jnp.float32, low / len(cuts), top_value / len(cuts)))
        level = level * jnp.repeat(heights, shape[dim] // parts).reshape([-1 if axis == dim else 1 for axis in range(len(shape))])
    return level


def centred(stream_key, shape, scale, limit, cuts=(), kind=jnp.bfloat16):
    array = jax.random.normal(stream_key, shape, jnp.float32) * scale
    if len(cuts) > 0:
        array = shard_levels(stream_key, shape, cuts, -0.22, 0.18) * array
    return jnp.clip(array, min=-limit, max=limit).astype(kind)


def setup_inputs(seed: int = 0) -> dict:
    splits = jax.random.split(jax.random.key(seed), 5)
    return {
        "embeddings": centred(splits[0], (ROWS_ALL, D), 0.03125, 0.25, ((0, 256),)),
        "assignments": draw_assignments(jax.random.fold_in(splits[4], 71), 0),
        "old_centroids": centred(splits[2], (CLUSTERS, D), 0.03125, 0.25, ((0, 64),)),
        "prior_counts": place_ends(jax.random.randint(splits[3], (CLUSTERS,), 1, 9), jax.random.fold_in(splits[3], 1), 1, 8).astype(jnp.int32),
    }


def reference(embeddings, assignments, old_centroids, prior_counts):
    values = embeddings.astype(jnp.float32)
    sums = jax.ops.segment_sum(values, assignments, num_segments=CLUSTERS)
    counts = jax.ops.segment_sum(jnp.ones(assignments.shape, jnp.float32), assignments, num_segments=CLUSTERS)
    prior = prior_counts.astype(jnp.float32)
    total = prior + counts
    mean = (prior[:, None] * old_centroids.astype(jnp.float32) + sums) / total[:, None]
    scale = lax.rsqrt(lax.optimization_barrier(jnp.sum(mean * mean, axis=1, keepdims=True)) + 1e-06)
    centroids = (mean * scale).astype(jnp.bfloat16)
    weight = (1.0 / total).astype(jnp.bfloat16)
    near = centroids[assignments].astype(jnp.float32)
    diff = values - near
    dist = lax.optimization_barrier(jnp.sum(diff * diff, axis=1))
    row_score = weight[assignments].astype(jnp.float32) * dist
    return (centroids, row_score)
```

```python
import functools

import jax
import jax.numpy as jnp
from jax import lax
from jax.experimental import pallas as pl
from jax.experimental.pallas import tpu as pltpu
from jax.sharding import PartitionSpec as P

MESH = pl.DeviceIdType.MESH
F32, BF16, I32 = jnp.float32, jnp.bfloat16, jnp.int32
LANES = 128
NT = (((1,), (1,)), ((), ()))
TN = (((0,), (0,)), ((), ()))


def displacements(planes, columns):
    z_order = []
    for step in range(planes // 2, 0, -1):
        z_order += [step, planes - step] if step != planes - step else [step]
    half = len(z_order) // 2
    z_order = [z for pair in zip(z_order[:half], z_order[half:]) for z in pair] + z_order[2 * half :]
    z_order.append(0)
    order = [
        (z_order[i % planes], (i // planes + i) % columns, (i // (planes * columns) + i) % 2)
        for i in range(planes * columns * 2)
    ]
    assert len(set(order)) == planes * columns * 2
    return [one for one in order if one != (0, 0, 0)]


def bf(mask):
    return jnp.where(mask, 1.0, 0.0).astype(BF16)


def kernel(
    owners, copies, cap, chunks,
    emb_ref, assign_ref, old_ref, prior_ref,
    cent_ref, score_ref,
    out, arr, pick, pick_t, part, rs_in, mean, acc, old, total_b, prior_b, weight_b, sumsq,
    ids_out, ids_in, cnt, sc_out, sc_in,
    send_sem, recv_sem, ids_sem, cnt_sem, rs_sem, ag_sem, sc_sem, old_sem,
):
    rows_here, width = emb_ref.shape
    per_owner = old_ref.shape[0]
    slots = owners * cap
    wide = width // chunks
    quarter = per_owner // copies
    me, rep = lax.axis_index("rows"), lax.axis_index("rep")
    columns = 4
    planes = owners // (2 * columns)
    z, x, core = me // (2 * columns), (me // 2) % columns, me % 2
    peers = [
        ((z + dz) % planes) * (2 * columns) + ((x + dx) % columns) * 2 + (core + dc) % 2
        for dz, dx, dc in displacements(planes, columns)
    ]
    mates = [lax.rem(rep + d, copies) for d in range(1, copies)]

    old_copy = pltpu.make_async_copy(old_ref, old, old_sem)
    old_copy.start()

    barrier = pltpu.get_barrier_semaphore()
    for peer in peers:
        pl.semaphore_signal(barrier, inc=1, device_id={"rows": peer}, device_id_type=MESH)
    for mate in mates:
        pl.semaphore_signal(barrier, inc=1, device_id={"rep": mate}, device_id_type=MESH)

    assign = assign_ref[...]
    owner_row = assign // per_owner
    local_row = assign - owner_row * per_owner
    owner_col = lax.broadcasted_iota(I32, (owners, rows_here), 0)
    mine = owner_row == owner_col
    starts = jnp.sum(jnp.where(owner_row < owner_col, 1.0, 0.0), axis=1, keepdims=True)
    start_row = jnp.sum(jnp.where(mine, starts, 0.0), axis=0, keepdims=True).astype(I32)
    rank_row = lax.broadcasted_iota(I32, (1, rows_here), 1) - start_row
    slot_row = owner_row * cap + rank_row

    code = local_row + 1
    at_rank = lax.broadcasted_iota(I32, (LANES, rows_here), 0) == rank_row
    high = jnp.where(at_rank, code // 32, 0).astype(F32).astype(BF16)
    low = jnp.where(at_rank, code % 32, 0).astype(F32).astype(BF16)
    mine_b = bf(mine)
    code_out = 32.0 * lax.dot_general(mine_b, high, NT, preferred_element_type=F32)
    code_out += lax.dot_general(mine_b, low, NT, preferred_element_type=F32)
    ids_out[...] = code_out.astype(I32).reshape(owners, 1, LANES)

    block = 256
    for b in range(slots // block):
        s = lax.broadcasted_iota(I32, (block, rows_here), 0) + b * block
        pick[b * block : (b + 1) * block, :] = bf(s == slot_row)

    pl.semaphore_wait(barrier, len(peers) + len(mates))

    ids_in[pl.ds(me, 1)] = ids_out[pl.ds(me, 1)]
    for peer in peers:
        pltpu.make_async_remote_copy(
            src_ref=ids_out.at[pl.ds(peer, 1)],
            dst_ref=ids_in.at[pl.ds(me, 1)],
            send_sem=ids_sem.at[0],
            recv_sem=ids_sem.at[1],
            device_id={"rows": peer},
            device_id_type=MESH,
        ).start()

    def fill(c):
        cols = pl.ds(pl.multiple_of(c * wide, wide), wide)
        out[c] = jnp.dot(pick[...], emb_ref[:, cols], preferred_element_type=F32).astype(BF16)
        here = pl.ds(pl.multiple_of(me * cap, cap), cap)
        arr[c, here, :] = out[c, here, :]

    def send(c):
        for peer in peers:
            pltpu.make_async_remote_copy(
                src_ref=out.at[c, pl.ds(pl.multiple_of(peer * cap, cap), cap), :],
                dst_ref=arr.at[c, pl.ds(pl.multiple_of(me * cap, cap), cap), :],
                send_sem=send_sem.at[c],
                recv_sem=recv_sem.at[c],
                device_id={"rows": peer},
                device_id_type=MESH,
            ).start()

    ahead = 2

    @pl.loop(0, chunks)
    def _(c):
        fill(c)

        @pl.when(c < ahead)
        def _():
            send(c)

    def landed(ref, sem):
        pltpu.make_async_copy(ref, ref, sem).wait()

    others = owners - 1
    landed(ids_in.at[0:others], ids_sem.at[1])
    landed(ids_out.at[0:others], ids_sem.at[0])

    codes = ids_in[...].reshape(owners, 1, LANES)
    spread = jnp.broadcast_to(codes, (owners, cap, LANES)).reshape(slots, LANES)
    lane = lax.broadcasted_iota(I32, (slots, LANES), 1)
    place = lax.broadcasted_iota(I32, (slots, LANES), 0) % cap
    id_col = jnp.sum(jnp.where(lane == place, spread, 0).astype(F32), axis=1, keepdims=True) - 1.0
    id_wide = jnp.broadcast_to(id_col, (slots, LANES))
    id_row = id_wide.T[0:1, :].astype(I32)
    id_col = id_col.astype(I32)
    for b in range(slots // block):
        k = lax.broadcasted_iota(I32, (block, per_owner), 1)
        pick[b * block : (b + 1) * block, :] = bf(k == id_col[b * block : (b + 1) * block, :])
    for b in range(per_owner // block):
        k = lax.broadcasted_iota(I32, (block, slots), 0) + b * block
        pick_t[b * block : (b + 1) * block, :] = bf(k == id_row)

    cnt[0] = jnp.dot(jnp.ones((8, slots), BF16), pick[...], preferred_element_type=F32)
    for d, mate in enumerate(mates):
        pltpu.make_async_remote_copy(
            src_ref=cnt.at[0], dst_ref=cnt.at[d + 1], send_sem=cnt_sem.at[0], recv_sem=cnt_sem.at[1],
            device_id={"rep": mate}, device_id_type=MESH,
        ).start()
    landed(cnt.at[1:copies], cnt_sem.at[1])
    landed(cnt.at[1:copies], cnt_sem.at[0])
    prior_row = prior_ref[...].astype(F32)
    counts = cnt[0, 0:1, :]
    for d in range(1, copies):
        counts += cnt[d, 0:1, :]
    total_row = prior_row + counts
    total_b[...] = jnp.broadcast_to(total_row, (LANES, per_owner)).T
    prior_b[...] = jnp.broadcast_to(prior_row, (LANES, per_owner)).T
    weight_row = jnp.broadcast_to((1.0 / total_row).astype(BF16), (LANES, per_owner))
    weight_b[...] = lax.dot_general(pick[...], weight_row, NT, preferred_element_type=F32)
    sumsq[...] = jnp.zeros_like(sumsq)
    acc[...] = jnp.zeros_like(acc)
    old_copy.wait()

    def quarter_of(q):
        return pl.ds(pl.multiple_of(q * quarter, quarter), quarter)

    def scatter(c):
        for d, mate in enumerate(mates):
            pltpu.make_async_remote_copy(
                src_ref=part.at[c, quarter_of(mate), :],
                dst_ref=rs_in.at[c, d],
                send_sem=rs_sem.at[0, c], recv_sem=rs_sem.at[1, c],
                device_id={"rep": mate}, device_id_type=MESH,
            ).start()

    def gather(c):
        landed(rs_in.at[c], rs_sem.at[1, c])
        own = quarter_of(rep)
        sums = part[c, own, :]
        for d in range(copies - 1):
            sums += rs_in[c, d]
        cols = pl.ds(pl.multiple_of(c * wide, wide), wide)
        was = old[own, cols].astype(F32)
        mean[c, own, :] = (prior_b[own, :] * was + sums) / total_b[own, :]
        for mate in mates:
            pltpu.make_async_remote_copy(
                src_ref=mean.at[c, own, :],
                dst_ref=mean.at[c, own, :],
                send_sem=ag_sem.at[0, c], recv_sem=ag_sem.at[1, c],
                device_id={"rep": mate}, device_id_type=MESH,
            ).start()

    def square(c):
        landed(rs_in.at[c], ag_sem.at[1, c])
        m = mean[c]
        sumsq[...] += m * m

    @pl.loop(0, chunks)
    def _(c):
        landed(arr.at[c, 0 : others * cap, :], recv_sem.at[c])

        @pl.when(c + ahead < chunks)
        def _():
            send(c + ahead)

        part[c] = jnp.dot(pick_t[...], arr[c], preferred_element_type=F32)
        scatter(c)

        @pl.when(c >= 1)
        def _():
            gather(c - 1)

        @pl.when(c >= 2)
        def _():
            square(c - 2)

    gather(chunks - 1)
    square(chunks - 2)
    square(chunks - 1)

    norm = jnp.sum(sumsq[...], axis=1, keepdims=True) + 1e-06
    sumsq[...] = jnp.broadcast_to(lax.rsqrt(norm), (per_owner, LANES))

    pair = 2

    @pl.loop(0, chunks // pair)
    def _(g):
        cols = pl.ds(pl.multiple_of(g * pair * wide, pair * wide), pair * wide)
        scaled = [(mean[g * pair + i] * sumsq[...]).astype(BF16) for i in range(pair)]
        cent_ref[:, cols] = jnp.concatenate(scaled, axis=1)
        near = jnp.dot(pick[...], cent_ref[:, cols], preferred_element_type=F32)
        for i in range(pair):
            diff = arr[g * pair + i].astype(F32) - near[:, i * wide : (i + 1) * wide]
            acc[...] += diff * diff

    dist = jnp.sum(acc[...], axis=1, keepdims=True)
    scores = weight_b[...] * dist
    scores = jnp.where(lane == place, scores, 0.0).reshape(owners, cap, LANES)
    sc_out[...] = jnp.sum(scores, axis=1, keepdims=True)
    sc_in[pl.ds(me, 1)] = sc_out[pl.ds(me, 1)]
    for peer in peers:
        pltpu.make_async_remote_copy(
            src_ref=sc_out.at[pl.ds(peer, 1)],
            dst_ref=sc_in.at[pl.ds(me, 1)],
            send_sem=sc_sem.at[0], recv_sem=sc_sem.at[1],
            device_id={"rows": peer}, device_id_type=MESH,
        ).start()
    landed(sc_in.at[0:others], sc_sem.at[1])
    back = sc_in[...].reshape(owners, LANES)
    mine_f = jnp.where(mine, 1.0, 0.0)
    found = lax.dot_general(
        back, mine_f, TN, precision=lax.Precision.HIGHEST, preferred_element_type=F32
    )
    score_ref[...] = jnp.sum(jnp.where(at_rank, found, 0.0), axis=0, keepdims=True)

    landed(sc_out.at[0:others], sc_sem.at[0])

    @pl.loop(0, chunks)
    def _(c):
        landed(out.at[c, 0 : others * cap, :], send_sem.at[c])
        landed(rs_in.at[c], rs_sem.at[0, c])
        landed(rs_in.at[c], ag_sem.at[0, c])


def on_device(embeddings, assignments, old_centroids, prior_counts):
    rows_here, width = embeddings.shape
    owners, copies = lax.axis_size("rows"), lax.axis_size("rep")
    per_owner = old_centroids.shape[0]
    cap = 2 * rows_here // owners
    slots = owners * cap
    chunks = width // LANES
    wide = LANES
    quarter = per_owner // copies
    vmem = pl.BlockSpec(memory_space=pltpu.VMEM)
    dma = pltpu.SemaphoreType.DMA
    centroids, row_score = pl.pallas_call(
        functools.partial(kernel, owners, copies, cap, chunks),
        out_shape=(
            jax.ShapeDtypeStruct((per_owner, width), BF16),
            jax.ShapeDtypeStruct((1, rows_here), F32),
        ),
        in_specs=[vmem, vmem, pl.BlockSpec(memory_space=pl.ANY), vmem],
        out_specs=(vmem, vmem),
        scratch_shapes=[
            pltpu.VMEM((chunks, slots, wide), BF16),
            pltpu.VMEM((chunks, slots, wide), BF16),
            pltpu.VMEM((slots, per_owner), BF16),
            pltpu.VMEM((per_owner, slots), BF16),
            pltpu.VMEM((chunks, per_owner, wide), F32),
            pltpu.VMEM((chunks, copies - 1, quarter, wide), F32),
            pltpu.VMEM((chunks, per_owner, wide), F32),
            pltpu.VMEM((slots, LANES), F32),
            pltpu.VMEM((per_owner, width), BF16),
            pltpu.VMEM((per_owner, LANES), F32),
            pltpu.VMEM((per_owner, LANES), F32),
            pltpu.VMEM((slots, LANES), F32),
            pltpu.VMEM((per_owner, LANES), F32),
            pltpu.VMEM((owners, 1, LANES), I32),
            pltpu.VMEM((owners, 1, LANES), I32),
            pltpu.VMEM((copies, 8, per_owner), F32),
            pltpu.VMEM((owners, 1, LANES), F32),
            pltpu.VMEM((owners, 1, LANES), F32),
            dma((chunks,)), dma((chunks,)), dma((2,)), dma((2,)),
            dma((2, chunks)), dma((2, chunks)), dma((2,)), dma,
        ],
        compiler_params=pltpu.CompilerParams(
            collective_id=0, has_side_effects=True, vmem_limit_bytes=60 * 2**20
        ),
        name="centroid_step",
    )(embeddings, assignments.reshape(1, rows_here), old_centroids, prior_counts.reshape(1, per_owner))
    return centroids, row_score.reshape(rows_here)


def solution(mesh):
    placed = (P(("rows", "rep"), None), P(("rows", "rep")), P("rows", None), P("rows"))
    return jax.shard_map(
        on_device,
        mesh=mesh,
        in_specs=placed,
        out_specs=(P("rows", None), P(("rows", "rep"))),
        check_vma=False,
    )
```

```python
import functools

import jax
import jax.numpy as jnp
from jax import lax
from jax.experimental import pallas as pl
from jax.experimental.pallas import tpu as pltpu
from jax.sharding import PartitionSpec as P

MESH = pl.DeviceIdType.MESH
F32, BF16, I32 = jnp.float32, jnp.bfloat16, jnp.int32
LANES = 128
NT = (((1,), (1,)), ((), ()))
TN = (((0,), (0,)), ((), ()))


def displacements(planes, columns):
    z_order = []
    for step in range(planes // 2, 0, -1):
        z_order += [step, planes - step] if step != planes - step else [step]
    half = len(z_order) // 2
    z_order = [z for pair in zip(z_order[:half], z_order[half:]) for z in pair] + z_order[2 * half :]
    z_order.append(0)
    order = [
        (z_order[i % planes], (i // planes + i) % columns, (i // (planes * columns) + i) % 2)
        for i in range(planes * columns * 2)
    ]
    assert len(set(order)) == planes * columns * 2
    return [one for one in order if one != (0, 0, 0)]


def bf(mask):
    return jnp.where(mask, 1.0, 0.0).astype(BF16)


def kernel(
    owners, copies, cap, chunks, late,
    emb_hbm, assign_ref, old_ref, prior_ref,
    cent_ref, score_ref,
    emb, out, arr, pick, pick_t, part, rs_in, mean, cent, acc, old, total_b, prior_b, weight_b,
    sumsq, scale, scale_msg,
    ids_out, ids_in, cnt, sc_out, sc_in,
    send_sem, recv_sem, ids_sem, cnt_sem, rs_sem, ag_sem, scale_sem, sc_sem, old_sem, emb_sem,
    cent_sem,
):
    rows_here, width = emb.shape
    per_owner = old.shape[0]
    slots = owners * cap
    wide = width // chunks
    quarter = per_owner // copies
    me, rep = lax.axis_index("rows"), lax.axis_index("rep")
    columns = 4
    planes = owners // (2 * columns)
    z, x, core = me // (2 * columns), (me // 2) % columns, me % 2
    peers = [
        ((z + dz) % planes) * (2 * columns) + ((x + dx) % columns) * 2 + (core + dc) % 2
        for dz, dx, dc in displacements(planes, columns)
    ]
    mates = [lax.rem(rep + d, copies) for d in range(1, copies)]
    others = owners - 1

    emb_copy = pltpu.make_async_copy(emb_hbm, emb, emb_sem)
    emb_copy.start()

    barrier = pltpu.get_barrier_semaphore()
    for peer in peers:
        pl.semaphore_signal(barrier, inc=1, device_id={"rows": peer}, device_id_type=MESH)
    for mate in mates:
        pl.semaphore_signal(barrier, inc=1, device_id={"rep": mate}, device_id_type=MESH)

    old_copy = pltpu.make_async_copy(old_ref, old, old_sem)
    old_copy.start()

    def landed(ref, sem):
        pltpu.make_async_copy(ref, ref, sem).wait()

    def tell(src, dst, sems, **where):
        pltpu.make_async_remote_copy(
            src_ref=src, dst_ref=dst, send_sem=sems[0], recv_sem=sems[1],
            device_id=where, device_id_type=MESH,
        ).start()

    def columns_of(c, n=1):
        return pl.ds(pl.multiple_of(c * wide, wide), n * wide)

    def slots_of(owner):
        return pl.ds(pl.multiple_of(owner * cap, cap), cap)

    def quarter_of(q):
        return pl.ds(pl.multiple_of(q * quarter, quarter), quarter)

    assign = assign_ref[...]
    owner_row = assign // per_owner
    local_row = assign - owner_row * per_owner
    owner_col = lax.broadcasted_iota(I32, (owners, rows_here), 0)
    mine = owner_row == owner_col
    starts = jnp.sum(jnp.where(owner_row < owner_col, 1.0, 0.0), axis=1, keepdims=True)
    start_row = jnp.sum(jnp.where(mine, starts, 0.0), axis=0, keepdims=True).astype(I32)
    rank_row = lax.broadcasted_iota(I32, (1, rows_here), 1) - start_row
    slot_row = owner_row * cap + rank_row

    block = 256
    for b in range(slots // block):
        s = lax.broadcasted_iota(I32, (block, rows_here), 0) + b * block
        pick[b * block : (b + 1) * block, :] = bf(s == slot_row)

    def fill(c):
        out[c] = jnp.dot(pick[...], emb[:, columns_of(c)], preferred_element_type=F32).astype(BF16)
        arr[c, slots_of(me), :] = out[c, slots_of(me), :]

    def send(c):
        for peer in peers:
            tell(
                out.at[c, slots_of(peer), :], arr.at[c, slots_of(me), :],
                (send_sem.at[c], recv_sem.at[c]), rows=peer,
            )

    emb_copy.wait()
    fill(0)
    pl.semaphore_wait(barrier, len(peers) + len(mates))
    send(0)

    code = local_row + 1
    at_rank = lax.broadcasted_iota(I32, (LANES, rows_here), 0) == rank_row
    high = jnp.where(at_rank, code // 32, 0).astype(F32).astype(BF16)
    low = jnp.where(at_rank, code % 32, 0).astype(F32).astype(BF16)
    mine_b = bf(mine)
    code_out = 32.0 * lax.dot_general(mine_b, high, NT, preferred_element_type=F32)
    code_out += lax.dot_general(mine_b, low, NT, preferred_element_type=F32)
    ids_out[...] = code_out.astype(I32).reshape(owners, 1, LANES)
    ids_in[pl.ds(me, 1)] = ids_out[pl.ds(me, 1)]
    for peer in peers:
        tell(ids_out.at[pl.ds(peer, 1)], ids_in.at[pl.ds(me, 1)], (ids_sem.at[0], ids_sem.at[1]), rows=peer)

    ahead = 3

    @pl.loop(1, chunks)
    def _(c):
        fill(c)

        @pl.when(c < ahead)
        def _():
            send(c)

    landed(ids_in.at[0:others], ids_sem.at[1])
    landed(ids_out.at[0:others], ids_sem.at[0])

    codes = ids_in[...].reshape(owners, 1, LANES)
    spread = jnp.broadcast_to(codes, (owners, cap, LANES)).reshape(slots, LANES)
    lane = lax.broadcasted_iota(I32, (slots, LANES), 1)
    place = lax.broadcasted_iota(I32, (slots, LANES), 0) % cap
    id_col = jnp.sum(jnp.where(lane == place, spread, 0).astype(F32), axis=1, keepdims=True) - 1.0
    id_wide = jnp.broadcast_to(id_col, (slots, LANES))
    id_row = id_wide.T[0:1, :].astype(I32)
    id_col = id_col.astype(I32)
    for b in range(slots // block):
        k = lax.broadcasted_iota(I32, (block, per_owner), 1)
        pick[b * block : (b + 1) * block, :] = bf(k == id_col[b * block : (b + 1) * block, :])
    for b in range(per_owner // block):
        k = lax.broadcasted_iota(I32, (block, slots), 0) + b * block
        pick_t[b * block : (b + 1) * block, :] = bf(k == id_row)

    cnt[0] = jnp.dot(jnp.ones((8, slots), BF16), pick[...], preferred_element_type=F32)
    for d, mate in enumerate(mates):
        tell(cnt.at[0], cnt.at[d + 1], (cnt_sem.at[0], cnt_sem.at[1]), rep=mate)
    landed(cnt.at[1:copies], cnt_sem.at[1])
    landed(cnt.at[1:copies], cnt_sem.at[0])
    prior_row = prior_ref[...].astype(F32)
    counts = cnt[0, 0:1, :]
    for d in range(1, copies):
        counts += cnt[d, 0:1, :]
    total_row = prior_row + counts
    total_b[...] = jnp.broadcast_to(total_row, (LANES, per_owner)).T
    prior_b[...] = jnp.broadcast_to(prior_row, (LANES, per_owner)).T
    weight_row = jnp.broadcast_to((1.0 / total_row).astype(BF16), (LANES, per_owner))
    weight_b[...] = lax.dot_general(pick[...], weight_row, NT, preferred_element_type=F32)
    sumsq[...] = jnp.zeros_like(sumsq)
    acc[...] = jnp.zeros_like(acc)
    old_copy.wait()
    own = quarter_of(rep)

    def partial(c, q):
        part[c, quarter_of(q), :] = jnp.dot(
            pick_t[quarter_of(q), :], arr[c], preferred_element_type=F32
        )

    def settle(c):
        landed(rs_in.at[c], rs_sem.at[1, c])
        sums = part[c, own, :]
        for d in range(copies - 1):
            sums += rs_in[c, d]
        was = old[own, columns_of(c)].astype(F32)
        here = (prior_b[own, :] * was + sums) / total_b[own, :]
        mean[c, own, :] = here
        sumsq[...] += here * here

    def share(c):
        for mate in mates:
            tell(mean.at[c, own, :], mean.at[c, own, :], (ag_sem.at[0, c], ag_sem.at[1, c]), rep=mate)

    @pl.loop(0, chunks)
    def _(c):
        landed(arr.at[c, 0 : others * cap, :], recv_sem.at[c])

        @pl.when(c + ahead < chunks)
        def _():
            send(c + ahead)

        for d in (1, 0, 2):
            partial(c, mates[d])
            tell(
                part.at[c, quarter_of(mates[d]), :], rs_in.at[c, d],
                (rs_sem.at[0, c], rs_sem.at[1, c]), rep=mates[d],
            )
        partial(c, rep)

        @pl.when(c >= 1)
        def _():
            settle(c - 1)

        @pl.when(jnp.logical_and(c >= 1, c <= chunks - late))
        def _():
            share(c - 1)

    settle(chunks - 1)
    norm = jnp.sum(sumsq[...], axis=1, keepdims=True) + 1e-06
    scale_own = jnp.broadcast_to(lax.rsqrt(norm), (quarter, LANES))
    scale_msg[rep] = scale_own.T[0:8, :]
    for mate in mates:
        tell(scale_msg.at[rep], scale_msg.at[rep], (scale_sem.at[0], scale_sem.at[1]), rep=mate)
    for c in range(chunks - late, chunks):
        cent[c, own, :] = (mean[c, own, :] * scale_own).astype(BF16)
        for mate in mates:
            tell(cent.at[c, own, :], cent.at[c, own, :], (ag_sem.at[0, c], ag_sem.at[1, c]), rep=mate)
    landed(scale_msg.at[0 : copies - 1], scale_sem.at[1])
    for q in range(copies):
        scale[q * quarter : (q + 1) * quarter, :] = jnp.broadcast_to(
            scale_msg[q, 0:1, :], (LANES, quarter)
        ).T

    def write_out(c):
        return pltpu.make_async_copy(cent.at[c], cent_ref.at[:, columns_of(c)], cent_sem.at[c])

    def finish(c):
        landed(rs_in.at[c], ag_sem.at[1, c])
        cent[c] = (mean[c] * scale[...]).astype(BF16)
        write_out(c).start()

    def both(c):
        return jnp.concatenate([cent[c], cent[c + 1]], axis=1)

    def gap(c, where, near):
        one = arr[c, where, :].astype(F32) - near[:, 0:wide]
        two = arr[c + 1, where, :].astype(F32) - near[:, wide:]
        return one * one + two * two

    @pl.loop(0, chunks // 2 - 1)
    def _(g):
        finish(2 * g)
        finish(2 * g + 1)
        near = jnp.dot(pick[...], both(2 * g), preferred_element_type=F32)
        acc[...] += gap(2 * g, slice(None), near)

    for c in range(chunks - 2, chunks):
        if c < chunks - late:
            finish(c)
        else:
            landed(cent.at[c, 0 : per_owner - quarter, :], ag_sem.at[1, c])
            write_out(c).start()

    groups = 4
    held = owners // groups
    span = held * cap
    here_lane = lax.broadcasted_iota(I32, (span, LANES), 1)
    here_place = lax.broadcasted_iota(I32, (span, LANES), 0) % cap
    sc_sems = (sc_sem.at[0], sc_sem.at[1])
    for turn in (2, 1, 3, 0):
        first = lax.rem(me // held + turn, groups) * held
        where = pl.ds(pl.multiple_of(first * cap, span), span)
        near = jnp.dot(pick[where, :], both(chunks - 2), preferred_element_type=F32)
        dist = jnp.sum(acc[where, :] + gap(chunks - 2, where, near), axis=1, keepdims=True)
        scores = weight_b[where, :] * dist
        scores = jnp.where(here_lane == here_place, scores, 0.0).reshape(held, cap, LANES)
        sc_out[pl.ds(first, held)] = jnp.sum(scores, axis=1, keepdims=True)
        for j in range(1 if turn == 0 else 0, held):
            peer = first + (lax.rem(me + j, held) if turn == 0 else j)
            tell(sc_out.at[pl.ds(peer, 1)], sc_in.at[pl.ds(me, 1)], sc_sems, rows=peer)
    sc_in[pl.ds(me, 1)] = sc_out[pl.ds(me, 1)]

    @pl.loop(0, chunks)
    def _(c):
        landed(out.at[c, 0 : others * cap, :], send_sem.at[c])
        landed(rs_in.at[c], rs_sem.at[0, c])
        write_out(c).wait()

    for c in range(chunks):
        if c < chunks - late:
            landed(rs_in.at[c], ag_sem.at[0, c])
        else:
            landed(cent.at[c, 0 : per_owner - quarter, :], ag_sem.at[0, c])
    landed(scale_msg.at[0 : copies - 1], scale_sem.at[0])

    landed(sc_in.at[0:others], sc_sem.at[1])
    back = sc_in[...].reshape(owners, LANES)
    found = lax.dot_general(
        back, jnp.where(mine, 1.0, 0.0), TN, precision=lax.Precision.HIGHEST, preferred_element_type=F32
    )
    score_ref[...] = jnp.sum(jnp.where(at_rank, found, 0.0), axis=0, keepdims=True)
    landed(sc_out.at[0:others], sc_sem.at[0])


def on_device(embeddings, assignments, old_centroids, prior_counts):
    rows_here, width = embeddings.shape
    owners, copies = lax.axis_size("rows"), lax.axis_size("rep")
    per_owner = old_centroids.shape[0]
    cap = 2 * rows_here // owners
    slots = owners * cap
    chunks = width // LANES
    wide = LANES
    quarter = per_owner // copies
    late = 2
    vmem = pl.BlockSpec(memory_space=pltpu.VMEM)
    dma = pltpu.SemaphoreType.DMA
    anywhere = pl.BlockSpec(memory_space=pl.ANY)
    centroids, row_score = pl.pallas_call(
        functools.partial(kernel, owners, copies, cap, chunks, late),
        out_shape=(
            jax.ShapeDtypeStruct((per_owner, width), BF16),
            jax.ShapeDtypeStruct((1, rows_here), F32),
        ),
        in_specs=[anywhere, vmem, anywhere, vmem],
        out_specs=(anywhere, vmem),
        scratch_shapes=[
            pltpu.VMEM((rows_here, width), BF16),
            pltpu.VMEM((chunks, slots, wide), BF16),
            pltpu.VMEM((chunks, slots, wide), BF16),
            pltpu.VMEM((slots, per_owner), BF16),
            pltpu.VMEM((per_owner, slots), BF16),
            pltpu.VMEM((chunks, per_owner, wide), F32),
            pltpu.VMEM((chunks, copies - 1, quarter, wide), F32),
            pltpu.VMEM((chunks, per_owner, wide), F32),
            pltpu.VMEM((chunks, per_owner, wide), BF16),
            pltpu.VMEM((slots, LANES), F32),
            pltpu.VMEM((per_owner, width), BF16),
            pltpu.VMEM((per_owner, LANES), F32),
            pltpu.VMEM((per_owner, LANES), F32),
            pltpu.VMEM((slots, LANES), F32),
            pltpu.VMEM((quarter, LANES), F32),
            pltpu.VMEM((per_owner, LANES), F32),
            pltpu.VMEM((copies, 8, quarter), F32),
            pltpu.VMEM((owners, 1, LANES), I32),
            pltpu.VMEM((owners, 1, LANES), I32),
            pltpu.VMEM((copies, 8, per_owner), F32),
            pltpu.VMEM((owners, 1, LANES), F32),
            pltpu.VMEM((owners, 1, LANES), F32),
            dma((chunks,)), dma((chunks,)), dma((2,)), dma((2,)),
            dma((2, chunks)), dma((2, chunks)), dma((2,)), dma((2,)), dma, dma, dma((chunks,)),
        ],
        compiler_params=pltpu.CompilerParams(
            collective_id=0, has_side_effects=True, vmem_limit_bytes=46 * 2**20
        ),
        name="centroid_step",
    )(*[
        pltpu.with_memory_space_constraint(one, pltpu.HBM)
        for one in (
            embeddings, assignments.reshape(1, rows_here), old_centroids,
            prior_counts.reshape(1, per_owner),
        )
    ])
    return centroids, row_score.reshape(rows_here)


def solution(mesh):
    placed = (P(("rows", "rep"), None), P(("rows", "rep")), P("rows", None), P("rows"))
    return jax.shard_map(
        on_device,
        mesh=mesh,
        in_specs=placed,
        out_specs=(P("rows", None), P(("rows", "rep"))),
        check_vma=False,
    )
```

```python
import functools

import jax
import jax.numpy as jnp
from jax import lax
from jax.experimental import pallas as pl
from jax.experimental.pallas import tpu as pltpu
from jax.sharding import PartitionSpec as P

MESH = pl.DeviceIdType.MESH
F32, BF16, I32 = jnp.float32, jnp.bfloat16, jnp.int32
LANES = 128
NT = (((1,), (1,)), ((), ()))
TN = (((0,), (0,)), ((), ()))


def displacements(planes, columns):
    z_order = []
    for step in range(planes // 2, 0, -1):
        z_order += [step, planes - step] if step != planes - step else [step]
    half = len(z_order) // 2
    z_order = [z for pair in zip(z_order[:half], z_order[half:]) for z in pair] + z_order[2 * half :]
    z_order.append(0)
    order = [
        (z_order[i % planes], (i // planes + i) % columns, (i // (planes * columns) + i) % 2)
        for i in range(planes * columns * 2)
    ]
    assert len(set(order)) == planes * columns * 2
    return [one for one in order if one != (0, 0, 0)]


def bf(mask):
    return jnp.where(mask, 1.0, 0.0).astype(BF16)


def kernel(
    owners, copies, cap, chunks, late,
    emb_hbm, assign_ref, old_ref, prior_ref,
    cent_ref, score_ref,
    emb, out, arr, pick, pick_t, part, rs_in, mean, cent, acc, old, total_b, prior_b, weight_b,
    sumsq, scale, scale_msg,
    ids_out, ids_in, cnt, sc_out, sc_in,
    send_sem, recv_sem, ids_sem, cnt_sem, rs_sem, ag_sem, scale_sem, sc_sem, old_sem, emb_sem,
    cent_sem,
):
    rows_here, width = emb.shape
    per_owner = old.shape[0]
    slots = owners * cap
    wide = width // chunks
    quarter = per_owner // copies
    me, rep = lax.axis_index("rows"), lax.axis_index("rep")
    columns = 4
    planes = owners // (2 * columns)
    z, x, core = me // (2 * columns), (me // 2) % columns, me % 2
    peers = [
        ((z + dz) % planes) * (2 * columns) + ((x + dx) % columns) * 2 + (core + dc) % 2
        for dz, dx, dc in displacements(planes, columns)
    ]
    mates = [lax.rem(rep + d, copies) for d in range(1, copies)]
    others = owners - 1

    emb_copy = pltpu.make_async_copy(emb_hbm, emb, emb_sem)
    emb_copy.start()

    barrier = pltpu.get_barrier_semaphore()
    for peer in peers:
        pl.semaphore_signal(barrier, inc=1, device_id={"rows": peer}, device_id_type=MESH)
    for mate in mates:
        pl.semaphore_signal(barrier, inc=1, device_id={"rep": mate}, device_id_type=MESH)

    old_copy = pltpu.make_async_copy(old_ref, old, old_sem)
    old_copy.start()

    def landed(ref, sem):
        pltpu.make_async_copy(ref, ref, sem).wait()

    def tell(src, dst, sems, **where):
        pltpu.make_async_remote_copy(
            src_ref=src, dst_ref=dst, send_sem=sems[0], recv_sem=sems[1],
            device_id=where, device_id_type=MESH,
        ).start()

    def columns_of(c, n=1):
        return pl.ds(pl.multiple_of(c * wide, wide), n * wide)

    def slots_of(owner):
        return pl.ds(pl.multiple_of(owner * cap, cap), cap)

    def quarter_of(q):
        return pl.ds(pl.multiple_of(q * quarter, quarter), quarter)

    assign = assign_ref[...]
    owner_row = assign // per_owner
    local_row = assign - owner_row * per_owner
    owner_col = lax.broadcasted_iota(I32, (owners, rows_here), 0)
    mine = owner_row == owner_col
    starts = jnp.sum(jnp.where(owner_row < owner_col, 1.0, 0.0), axis=1, keepdims=True)
    start_row = jnp.sum(jnp.where(mine, starts, 0.0), axis=0, keepdims=True).astype(I32)
    rank_row = lax.broadcasted_iota(I32, (1, rows_here), 1) - start_row
    slot_row = owner_row * cap + rank_row

    block = 256
    for b in range(slots // block):
        s = lax.broadcasted_iota(I32, (block, rows_here), 0) + b * block
        pick[b * block : (b + 1) * block, :] = bf(s == slot_row)

    def fill(c):
        out[c] = jnp.dot(pick[...], emb[:, columns_of(c)], preferred_element_type=F32).astype(BF16)
        arr[c, slots_of(me), :] = out[c, slots_of(me), :]

    def send(c):
        for peer in peers:
            tell(
                out.at[c, slots_of(peer), :], arr.at[c, slots_of(me), :],
                (send_sem.at[c], recv_sem.at[c]), rows=peer,
            )

    emb_copy.wait()
    fill(0)
    pl.semaphore_wait(barrier, len(peers) + len(mates))
    send(0)

    code = local_row + 1
    at_rank = lax.broadcasted_iota(I32, (LANES, rows_here), 0) == rank_row
    high = jnp.where(at_rank, code // 32, 0).astype(F32).astype(BF16)
    low = jnp.where(at_rank, code % 32, 0).astype(F32).astype(BF16)
    mine_b = bf(mine)
    code_out = 32.0 * lax.dot_general(mine_b, high, NT, preferred_element_type=F32)
    code_out += lax.dot_general(mine_b, low, NT, preferred_element_type=F32)
    ids_out[...] = code_out.astype(I32).reshape(owners, 1, LANES)
    ids_in[pl.ds(me, 1)] = ids_out[pl.ds(me, 1)]
    for peer in peers:
        tell(ids_out.at[pl.ds(peer, 1)], ids_in.at[pl.ds(me, 1)], (ids_sem.at[0], ids_sem.at[1]), rows=peer)

    ahead = 3

    @pl.loop(1, chunks)
    def _(c):
        fill(c)

        @pl.when(c < ahead)
        def _():
            send(c)

    landed(ids_in.at[0:others], ids_sem.at[1])
    landed(ids_out.at[0:others], ids_sem.at[0])

    codes = ids_in[...].reshape(owners, 1, LANES)
    spread = jnp.broadcast_to(codes, (owners, cap, LANES)).reshape(slots, LANES)
    lane = lax.broadcasted_iota(I32, (slots, LANES), 1)
    place = lax.broadcasted_iota(I32, (slots, LANES), 0) % cap
    id_col = jnp.sum(jnp.where(lane == place, spread, 0).astype(F32), axis=1, keepdims=True) - 1.0
    id_wide = jnp.broadcast_to(id_col, (slots, LANES))
    id_row = id_wide.T[0:1, :].astype(I32)
    id_col = id_col.astype(I32)
    for b in range(slots // block):
        k = lax.broadcasted_iota(I32, (block, per_owner), 1)
        pick[b * block : (b + 1) * block, :] = bf(k == id_col[b * block : (b + 1) * block, :])
    for b in range(per_owner // block):
        k = lax.broadcasted_iota(I32, (block, slots), 0) + b * block
        pick_t[b * block : (b + 1) * block, :] = bf(k == id_row)

    cnt[0] = jnp.dot(jnp.ones((8, slots), BF16), pick[...], preferred_element_type=F32)
    for d, mate in enumerate(mates):
        tell(cnt.at[0], cnt.at[d + 1], (cnt_sem.at[0], cnt_sem.at[1]), rep=mate)
    landed(cnt.at[1:copies], cnt_sem.at[1])
    landed(cnt.at[1:copies], cnt_sem.at[0])
    prior_row = prior_ref[...].astype(F32)
    counts = cnt[0, 0:1, :]
    for d in range(1, copies):
        counts += cnt[d, 0:1, :]
    total_row = prior_row + counts
    total_b[...] = jnp.broadcast_to(total_row, (LANES, per_owner)).T
    prior_b[...] = jnp.broadcast_to(prior_row, (LANES, per_owner)).T
    weight_row = jnp.broadcast_to((1.0 / total_row).astype(BF16), (LANES, per_owner))
    weight_b[...] = lax.dot_general(pick[...], weight_row, NT, preferred_element_type=F32)
    sumsq[...] = jnp.zeros_like(sumsq)
    acc[...] = jnp.zeros_like(acc)
    old_copy.wait()
    own = quarter_of(rep)

    def partial(c, q):
        part[c, quarter_of(q), :] = jnp.dot(
            pick_t[quarter_of(q), :], arr[c], preferred_element_type=F32
        )

    def settle(c):
        landed(rs_in.at[c], rs_sem.at[1, c])
        sums = part[c, own, :]
        for d in range(copies - 1):
            sums += rs_in[c, d]
        was = old[own, columns_of(c)].astype(F32)
        here = (prior_b[own, :] * was + sums) / total_b[own, :]
        mean[c, own, :] = here
        sumsq[...] += here * here

    def share(c):
        for mate in mates:
            tell(mean.at[c, own, :], mean.at[c, own, :], (ag_sem.at[0, c], ag_sem.at[1, c]), rep=mate)

    @pl.loop(0, chunks)
    def _(c):
        landed(arr.at[c, 0 : others * cap, :], recv_sem.at[c])

        @pl.when(c + ahead < chunks)
        def _():
            send(c + ahead)

        for d in (1, 0, 2):
            partial(c, mates[d])
            tell(
                part.at[c, quarter_of(mates[d]), :], rs_in.at[c, d],
                (rs_sem.at[0, c], rs_sem.at[1, c]), rep=mates[d],
            )
        partial(c, rep)

        @pl.when(c >= 1)
        def _():
            settle(c - 1)

        @pl.when(jnp.logical_and(c >= 1, c <= chunks - late))
        def _():
            share(c - 1)

    settle(chunks - 1)
    norm = jnp.sum(sumsq[...], axis=1, keepdims=True) + 1e-06
    scale_own = jnp.broadcast_to(lax.rsqrt(norm), (quarter, LANES))
    scale_msg[rep] = scale_own.T[0:8, :]
    for mate in mates:
        tell(scale_msg.at[rep], scale_msg.at[rep], (scale_sem.at[0], scale_sem.at[1]), rep=mate)
    for c in range(chunks - late, chunks):
        cent[c, own, :] = (mean[c, own, :] * scale_own).astype(BF16)
        for mate in (mates[1], mates[0], mates[2]):
            tell(cent.at[c, own, :], cent.at[c, own, :], (ag_sem.at[0, c], ag_sem.at[1, c]), rep=mate)
    landed(scale_msg.at[0 : copies - 1], scale_sem.at[1])
    for q in range(copies):
        scale[q * quarter : (q + 1) * quarter, :] = jnp.broadcast_to(
            scale_msg[q, 0:1, :], (LANES, quarter)
        ).T

    def write_out(c):
        return pltpu.make_async_copy(cent.at[c], cent_ref.at[:, columns_of(c)], cent_sem.at[c])

    def finish(c):
        landed(rs_in.at[c], ag_sem.at[1, c])
        cent[c] = (mean[c] * scale[...]).astype(BF16)
        write_out(c).start()

    def both(c):
        return jnp.concatenate([cent[c], cent[c + 1]], axis=1)

    def gap(c, where, near):
        one = arr[c, where, :].astype(F32) - near[:, 0:wide]
        two = arr[c + 1, where, :].astype(F32) - near[:, wide:]
        return one * one + two * two

    @pl.loop(0, chunks // 2 - 1)
    def _(g):
        finish(2 * g)
        finish(2 * g + 1)
        near = jnp.dot(pick[...], both(2 * g), preferred_element_type=F32)
        acc[...] += gap(2 * g, slice(None), near)

    def single(c, where):
        near = jnp.dot(pick[where, :], cent[c], preferred_element_type=F32)
        diff = arr[c, where, :].astype(F32) - near
        return diff * diff

    for c in range(chunks - 2, chunks):
        landed(cent.at[c, 0 : per_owner - quarter, :], ag_sem.at[1, c])
        write_out(c).start()
        if c < chunks - 1:
            acc[...] += single(c, slice(None))

    groups = 4
    held = owners // groups
    span = held * cap
    here_lane = lax.broadcasted_iota(I32, (span, LANES), 1)
    here_place = lax.broadcasted_iota(I32, (span, LANES), 0) % cap
    sc_sems = (sc_sem.at[0], sc_sem.at[1])
    for turn in (2, 1, 3, 0):
        first = lax.rem(me // held + turn, groups) * held
        where = pl.ds(pl.multiple_of(first * cap, span), span)
        dist = jnp.sum(acc[where, :] + single(chunks - 1, where), axis=1, keepdims=True)
        scores = weight_b[where, :] * dist
        scores = jnp.where(here_lane == here_place, scores, 0.0).reshape(held, cap, LANES)
        sc_out[pl.ds(first, held)] = jnp.sum(scores, axis=1, keepdims=True)
        for j in range(1 if turn == 0 else 0, held):
            peer = first + (lax.rem(me + j, held) if turn == 0 else j)
            tell(sc_out.at[pl.ds(peer, 1)], sc_in.at[pl.ds(me, 1)], sc_sems, rows=peer)
    sc_in[pl.ds(me, 1)] = sc_out[pl.ds(me, 1)]

    @pl.loop(0, chunks)
    def _(c):
        landed(out.at[c, 0 : others * cap, :], send_sem.at[c])
        landed(rs_in.at[c], rs_sem.at[0, c])
        write_out(c).wait()

    for c in range(chunks):
        if c < chunks - late:
            landed(rs_in.at[c], ag_sem.at[0, c])
        else:
            landed(cent.at[c, 0 : per_owner - quarter, :], ag_sem.at[0, c])
    landed(scale_msg.at[0 : copies - 1], scale_sem.at[0])

    landed(sc_in.at[0:others], sc_sem.at[1])
    back = sc_in[...].reshape(owners, LANES)
    found = lax.dot_general(
        back, jnp.where(mine, 1.0, 0.0), TN, precision=lax.Precision.HIGHEST, preferred_element_type=F32
    )
    score_ref[...] = jnp.sum(jnp.where(at_rank, found, 0.0), axis=0, keepdims=True)
    landed(sc_out.at[0:others], sc_sem.at[0])


def on_device(embeddings, assignments, old_centroids, prior_counts):
    rows_here, width = embeddings.shape
    owners, copies = lax.axis_size("rows"), lax.axis_size("rep")
    per_owner = old_centroids.shape[0]
    cap = 2 * rows_here // owners
    slots = owners * cap
    chunks = width // LANES
    wide = LANES
    quarter = per_owner // copies
    late = 2
    vmem = pl.BlockSpec(memory_space=pltpu.VMEM)
    dma = pltpu.SemaphoreType.DMA
    anywhere = pl.BlockSpec(memory_space=pl.ANY)
    centroids, row_score = pl.pallas_call(
        functools.partial(kernel, owners, copies, cap, chunks, late),
        out_shape=(
            jax.ShapeDtypeStruct((per_owner, width), BF16),
            jax.ShapeDtypeStruct((1, rows_here), F32),
        ),
        in_specs=[anywhere, vmem, anywhere, vmem],
        out_specs=(anywhere, vmem),
        scratch_shapes=[
            pltpu.VMEM((rows_here, width), BF16),
            pltpu.VMEM((chunks, slots, wide), BF16),
            pltpu.VMEM((chunks, slots, wide), BF16),
            pltpu.VMEM((slots, per_owner), BF16),
            pltpu.VMEM((per_owner, slots), BF16),
            pltpu.VMEM((chunks, per_owner, wide), F32),
            pltpu.VMEM((chunks, copies - 1, quarter, wide), F32),
            pltpu.VMEM((chunks, per_owner, wide), F32),
            pltpu.VMEM((chunks, per_owner, wide), BF16),
            pltpu.VMEM((slots, LANES), F32),
            pltpu.VMEM((per_owner, width), BF16),
            pltpu.VMEM((per_owner, LANES), F32),
            pltpu.VMEM((per_owner, LANES), F32),
            pltpu.VMEM((slots, LANES), F32),
            pltpu.VMEM((quarter, LANES), F32),
            pltpu.VMEM((per_owner, LANES), F32),
            pltpu.VMEM((copies, 8, quarter), F32),
            pltpu.VMEM((owners, 1, LANES), I32),
            pltpu.VMEM((owners, 1, LANES), I32),
            pltpu.VMEM((copies, 8, per_owner), F32),
            pltpu.VMEM((owners, 1, LANES), F32),
            pltpu.VMEM((owners, 1, LANES), F32),
            dma((chunks,)), dma((chunks,)), dma((2,)), dma((2,)),
            dma((2, chunks)), dma((2, chunks)), dma((2,)), dma((2,)), dma, dma, dma((chunks,)),
        ],
        compiler_params=pltpu.CompilerParams(
            collective_id=0, has_side_effects=True, vmem_limit_bytes=46 * 2**20
        ),
        name="centroid_step",
    )(*[
        pltpu.with_memory_space_constraint(one, pltpu.HBM)
        for one in (
            embeddings, assignments.reshape(1, rows_here), old_centroids,
            prior_counts.reshape(1, per_owner),
        )
    ])
    return centroids, row_score.reshape(rows_here)


def solution(mesh):
    placed = (P(("rows", "rep"), None), P(("rows", "rep")), P("rows", None), P("rows"))
    return jax.shard_map(
        on_device,
        mesh=mesh,
        in_specs=placed,
        out_specs=(P("rows", None), P(("rows", "rep"))),
        check_vma=False,
    )
```
